128 devices in a mesh: clus: 8 (over x, core), trow: 4 (over y), tcol: 4 (over z).
Axes of the slice: x: 4, y: 4, z: 4, core: 2. Of those that a mesh axis runs over, the one named last changes fastest.
Arguments:
- embeddings: bfloat16 [65536, 1024], P(('clus', 'trow', 'tcol'))
- target: int32 [65536], P(('clus', 'trow', 'tcol')), may hold values from 0 to 98303, as said below
Outputs:
- best_cosine: float32 [65536], P(('clus', 'trow', 'tcol'))
The draws below stay inside these ranges and needn't reach their ends.
Inputs may be any that keep to these rules, and one draw needn't show every extreme that they name: `target`: the grid has 8 clusters of 12288 slots each; the rows of a cluster fill its slots 0 to its size - 1, each slot once; every cluster has a row, and the last cluster is the largest and fills all 12288 slots. The rows of one device send at most 6 rows to any aligned block of 768 slots, and some block receives exactly 6 from every device.
All inputs are finite; a program needn't handle non-finite values.
Results may differ from the reference program's by a relative error of at most 0.00069.
Values may be sent and summed in bfloat16 or wider, within the bound.
A program may use at most 128 MiB of HBM per device.

```python
import math
import jax
import jax.numpy as jnp
from jax import lax

D = 1024
R_IN = 512
CAP = 12288
CLUSTERS = 8
ROWS = 65536


def placement(key):
    base = jax.random.fold_in(key, 17)
    key_weights = jax.random.fold_in(base, 1)
    key_devices = jax.random.fold_in(base, 2)
    key_local = jax.random.fold_in(base, 3)
    devices = ROWS // R_IN
    labels = jnp.arange(CLUSTERS, dtype=jnp.int32)
    largest = CLUSTERS - 1
    weights = jnp.where(labels == largest, 0, jax.random.randint(key_weights, (CLUSTERS,), 2, 4))
    remaining = ROWS - CAP
    shares = remaining * weights // jnp.sum(weights)
    first_other = 0
    shares = shares + jnp.where(labels == first_other, remaining - jnp.sum(shares), 0)
    cluster_sizes = jnp.where(labels == largest, CAP, shares).astype(jnp.int32)
    slot_index = jnp.arange(CLUSTERS * CAP, dtype=jnp.int32)
    occupied = slot_index % CAP < cluster_sizes[slot_index // CAP]
    filled = jnp.nonzero(occupied, size=ROWS)[0].astype(jnp.int32)
    ordinal = jnp.arange(ROWS, dtype=jnp.int32)
    device_label = jax.random.permutation(key_devices, devices).astype(jnp.int32)
    local_orders = jax.vmap(lambda subkey: jax.random.permutation(subkey, R_IN))(jax.random.split(key_local, devices)).astype(jnp.int32)
    source_device = device_label[ordinal % devices]
    source_row = source_device * R_IN + local_orders[source_device, ordinal // devices]
    target = jnp.zeros((ROWS,), jnp.int32).at[source_row].set(filled)
    return target


def pairing(key, target):
    key_order, key_keep = jax.random.split(jax.random.fold_in(key, 41), 2)
    cluster = target // CAP
    ranking = jax.random.permutation(key_order, ROWS).astype(jnp.int32)
    scores = cluster * ROWS + ranking
    order = jnp.argsort(scores, stable=True).astype(jnp.int32)
    sorted_index = jnp.arange(ROWS, dtype=jnp.int32)
    neighbour = order[jnp.bitwise_xor(sorted_index, 1)]
    same_cluster = cluster[order] == cluster[neighbour]
    keep_pair = jax.random.randint(key_keep, (ROWS // 2,), 0, 5) < 2
    linked_sorted = same_cluster & keep_pair[sorted_index // 2]
    pair_of_row = jnp.zeros((ROWS,), jnp.int32).at[order].set(sorted_index // 2)
    linked_row = jnp.zeros((ROWS,), jnp.bool_).at[order].set(linked_sorted)
    return (pair_of_row, linked_row)


def draw_target(key, part):
    return placement(key)


def draw_embeddings(key, part):
    target = placement(key)
    pair_of_row, linked_row = pairing(key, target)
    noise_key, shared_key, mixing_key = jax.random.split(jax.random.fold_in(key, 29), 3)
    noise = jax.random.normal(noise_key, (ROWS, D), jnp.float32)
    shared = jax.random.normal(shared_key, (ROWS // 2, D), jnp.float32)
    mixing = jnp.exp(jax.random.uniform(mixing_key, (ROWS // 2,), jnp.float32, math.log(0.15), math.log(2.5)))
    strength = jnp.where(linked_row, mixing[pair_of_row], 0.0)
    values = noise + strength[:, None] * shared[pair_of_row]
    return values.astype(jnp.bfloat16)


def setup_inputs(seed: int = 0) -> dict:
    keys = jax.random.split(jax.random.key(seed), 3)
    return {
        "embeddings": draw_embeddings(jax.random.fold_in(keys[2], 71), 0),
        "target": draw_target(jax.random.fold_in(keys[2], 71), 0),
    }


epsilon = 1e-06
span_rows = 1024

def reference(embeddings, target):
    values = embeddings.astype(jnp.float32)
    unit_rows = (values / jnp.sqrt(lax.optimization_barrier(jnp.sum(values * values, axis=1, keepdims=True)) + epsilon)).astype(jnp.bfloat16)
    total_slots = CLUSTERS * CAP
    slotted = jnp.zeros((total_slots, D), jnp.float32).at[target].set(unit_rows.astype(jnp.float32))
    occupied = jnp.zeros((total_slots,), jnp.bool_).at[target].set(True)

    def one_cluster(cluster):
        first_slot = (cluster * CAP).astype(jnp.int32)
        members = lax.dynamic_slice_in_dim(slotted, first_slot, CAP)
        present = lax.dynamic_slice_in_dim(occupied, first_slot, CAP)
        column_index = jnp.arange(CAP, dtype=jnp.int32)

        def one_span(first):
            section = lax.dynamic_slice_in_dim(members, first.astype(jnp.int32), span_rows)
            scores = jnp.dot(section, members.T, precision=lax.Precision.HIGHEST)
            row_index = first.astype(jnp.int32) + jnp.arange(span_rows, dtype=jnp.int32)
            keep = present[None, :] & (column_index[None, :] != row_index[:, None])
            return lax.optimization_barrier(jnp.max(jnp.where(keep, scores, -1.0), axis=1))
        starts = jnp.arange(CAP // span_rows, dtype=jnp.int32) * span_rows
        return lax.map(one_span, starts).reshape(CAP)
    best = lax.map(one_cluster, jnp.arange(CLUSTERS, dtype=jnp.int32)).reshape(total_slots)
    return best[target]
```

```python
import jax
import jax.numpy as jnp
from jax import lax
from jax.sharding import PartitionSpec as P

SLOTS = 768

epsilon = 1e-06
ABSENT = 4.0


def on_device(embeddings, target):
    width = embeddings.shape[1]
    clusters_count = lax.axis_size("clus")
    tile_rows = lax.axis_size("trow")
    tile_cols = lax.axis_size("tcol")
    group_count = tile_rows * tile_cols
    devices = clusters_count * group_count
    pair_rows = SLOTS // devices

    values = embeddings.astype(jnp.float32)
    unit_rows = (
        values / jnp.sqrt(jnp.sum(values * values, axis=1, keepdims=True) + epsilon)
    ).astype(jnp.bfloat16)

    destination = target // SLOTS
    onehot = (destination[:, None] == jnp.arange(devices, dtype=jnp.int32)[None, :]).astype(
        jnp.int32
    )
    position = jnp.sum(onehot * (jnp.cumsum(onehot, axis=0) - 1), axis=1)
    buffer_slot = destination * pair_rows + position
    outgoing = jnp.full((SLOTS, width), ABSENT, jnp.bfloat16).at[buffer_slot].set(unit_rows)
    arrived = lax.all_to_all(
        outgoing.reshape(devices, pair_rows, width),
        ("clus", "trow", "tcol"),
        split_axis=0,
        concat_axis=0,
        tiled=True,
    ).reshape(SLOTS, width)

    row_pos = lax.axis_index("trow")
    col_pos = lax.axis_index("tcol")
    row_block = lax.all_gather(arrived, "tcol", axis=0, tiled=True)
    col_block = lax.all_gather(arrived, "trow", axis=0, tiled=True)
    local = jnp.arange(SLOTS, dtype=jnp.int32)
    row_index = (
        (row_pos * tile_cols + jnp.arange(tile_cols, dtype=jnp.int32))[:, None] * SLOTS
        + local[None, :]
    ).reshape(-1)
    col_index = (
        (jnp.arange(tile_rows, dtype=jnp.int32) * tile_cols + col_pos)[:, None] * SLOTS
        + local[None, :]
    ).reshape(-1)
    present = col_block[:, 0].astype(jnp.float32) < 2.0
    scores = lax.dot_general(
        row_block, col_block, (((1,), (1,)), ((), ())), preferred_element_type=jnp.float32
    )
    keep = present[None, :] & (col_index[None, :] != row_index[:, None])
    partial = jnp.max(jnp.where(keep, scores, -1.0), axis=1)

    outbound = partial.reshape(tile_cols, devices, pair_rows).transpose(1, 0, 2)
    returned = lax.all_to_all(
        outbound,
        ("clus", "trow", "tcol"),
        split_axis=0,
        concat_axis=0,
        tiled=True,
    )
    best = jnp.max(
        returned.reshape(clusters_count, tile_rows, tile_cols, tile_cols, pair_rows), axis=2
    ).reshape(SLOTS)
    return best[buffer_slot]


def solution(mesh):
    in_specs = (P(("clus", "trow", "tcol"), None), P(("clus", "trow", "tcol")))
    out_specs = P(("clus", "trow", "tcol"))
    return jax.shard_map(
        on_device, mesh=mesh, in_specs=in_specs, out_specs=out_specs, check_vma=False
    )
```

```python
import jax
import jax.numpy as jnp
from jax import lax
from jax.sharding import PartitionSpec as P

SLOTS = 768

epsilon = 1e-06
ABSENT = 4.0
OFFSETS = (0, -1, 1, 2)


def shift(x, axis, n, step):
    return lax.ppermute(x, axis, [(i, (i + step) % n) for i in range(n)])


def ring_gather(chunk, axis):
    n = lax.axis_size(axis)
    half = chunk.shape[0] // 2
    from_left = shift(chunk, axis, n, 1)
    from_right = shift(chunk, axis, n, -1)
    far = jnp.concatenate(
        [shift(from_right[:half], axis, n, -1), shift(from_left[half:], axis, n, 1)], axis=0
    )
    return [chunk, from_left, from_right, far]


def block_max(rows, cols, self_block):
    scores = lax.dot_general(
        rows, cols, (((1,), (1,)), ((), ())), preferred_element_type=jnp.float32
    )
    keep = (cols[:, 0].astype(jnp.float32) < 2.0)[None, :]
    if self_block:
        index = jnp.arange(rows.shape[0], dtype=jnp.int32)
        keep = keep & (index[:, None] != index[None, :])
    return jnp.max(jnp.where(keep, scores, -1.0), axis=1)


def on_device(embeddings, target):
    width = embeddings.shape[1]
    clusters_count = lax.axis_size("clus")
    tile_rows = lax.axis_size("trow")
    tile_cols = lax.axis_size("tcol")
    group_count = tile_rows * tile_cols
    devices = clusters_count * group_count
    pair_rows = SLOTS // devices

    values = embeddings.astype(jnp.float32)
    unit_rows = (
        values / jnp.sqrt(jnp.sum(values * values, axis=1, keepdims=True) + epsilon)
    ).astype(jnp.bfloat16)

    destination = target // SLOTS
    onehot = (destination[:, None] == jnp.arange(devices, dtype=jnp.int32)[None, :]).astype(
        jnp.int32
    )
    position = jnp.sum(onehot * (jnp.cumsum(onehot, axis=0) - 1), axis=1)
    buffer_slot = destination * pair_rows + position
    outgoing = jnp.full((SLOTS, width), ABSENT, jnp.bfloat16).at[buffer_slot].set(unit_rows)
    arrived = lax.all_to_all(
        outgoing.reshape(devices, pair_rows, width),
        ("clus", "trow", "tcol"),
        split_axis=0,
        concat_axis=0,
        tiled=True,
    ).reshape(SLOTS, width)

    row_chunks = ring_gather(arrived, "tcol")
    col_chunks = ring_gather(arrived, "trow")
    partial = jnp.stack(
        [
            jnp.max(
                jnp.stack(
                    [
                        block_max(rows, cols, a == 0 and b == 0)
                        for b, cols in enumerate(col_chunks)
                    ]
                ),
                axis=0,
            )
            for a, rows in enumerate(row_chunks)
        ]
    )

    outbound = partial.reshape(len(OFFSETS), devices, pair_rows).transpose(1, 0, 2)
    returned = lax.all_to_all(
        outbound,
        ("clus", "trow", "tcol"),
        split_axis=0,
        concat_axis=0,
        tiled=True,
    ).reshape(clusters_count, tile_rows, tile_cols, len(OFFSETS), pair_rows)
    owners = []
    for owner in range(tile_cols):
        candidates = []
        for sender in range(tile_cols):
            j = [(sender + o) % tile_cols for o in OFFSETS].index(owner)
            candidates.append(returned[:, :, sender, j, :])
        owners.append(jnp.max(jnp.stack(candidates), axis=0))
    best = jnp.stack(owners, axis=2).reshape(SLOTS)
    return best[buffer_slot]


def solution(mesh):
    in_specs = (P(("clus", "trow", "tcol"), None), P(("clus", "trow", "tcol")))
    out_specs = P(("clus", "trow", "tcol"))
    return jax.shard_map(
        on_device, mesh=mesh, in_specs=in_specs, out_specs=out_specs, check_vma=False
    )
```

```python
import jax
import jax.numpy as jnp
from jax import lax
from jax.sharding import PartitionSpec as P

SLOTS = 768

epsilon = 1e-06
ABSENT = 4.0
OFFSETS = (0, -1, 1, 2)


def shift(x, axis, n, step):
    return lax.ppermute(x, axis, [(i, (i + step) % n) for i in range(n)])


def ring_gather(chunk, axis):
    n = lax.axis_size(axis)
    half = chunk.shape[0] // 2
    from_left = shift(chunk, axis, n, 1)
    from_right = shift(chunk, axis, n, -1)
    far = jnp.concatenate(
        [shift(from_right[:half], axis, n, -1), shift(from_left[half:], axis, n, 1)], axis=0
    )
    return [chunk, from_left, from_right, far]


def block_max(rows, cols, self_block):
    scores = lax.dot_general(
        rows, cols, (((1,), (1,)), ((), ())), preferred_element_type=jnp.float32
    )
    keep = (cols[:, 0].astype(jnp.float32) < 2.0)[None, :]
    if self_block:
        index = jnp.arange(rows.shape[0], dtype=jnp.int32)
        keep = keep & (index[:, None] != index[None, :])
    return jnp.max(jnp.where(keep, scores, -1.0), axis=1)


def on_device(embeddings, target):
    width = embeddings.shape[1]
    clusters_count = lax.axis_size("clus")
    tile_rows = lax.axis_size("trow")
    tile_cols = lax.axis_size("tcol")
    group_count = tile_rows * tile_cols
    devices = clusters_count * group_count
    pair_rows = SLOTS // devices

    values = embeddings.astype(jnp.float32)
    unit_rows = (
        values / jnp.sqrt(jnp.sum(values * values, axis=1, keepdims=True) + epsilon)
    ).astype(jnp.bfloat16)

    destination = target // SLOTS
    onehot = (destination[:, None] == jnp.arange(devices, dtype=jnp.int32)[None, :]).astype(
        jnp.int32
    )
    position = jnp.sum(onehot * (jnp.cumsum(onehot, axis=0) - 1), axis=1)
    buffer_slot = destination * pair_rows + position
    outgoing = jnp.full((SLOTS, width), ABSENT, jnp.bfloat16).at[buffer_slot].set(unit_rows)
    arrived = lax.all_to_all(
        outgoing.reshape(devices, pair_rows * width),
        ("clus", "trow", "tcol"),
        split_axis=0,
        concat_axis=0,
        tiled=True,
    ).reshape(SLOTS, width)

    row_chunks = ring_gather(arrived, "tcol")
    col_chunks = ring_gather(arrived, "trow")
    partial = jnp.stack(
        [
            jnp.max(
                jnp.stack(
                    [
                        block_max(rows, cols, a == 0 and b == 0)
                        for b, cols in enumerate(col_chunks)
                    ]
                ),
                axis=0,
            )
            for a, rows in enumerate(row_chunks)
        ]
    )

    outbound = partial.reshape(len(OFFSETS), devices, pair_rows).transpose(1, 0, 2)
    returned = lax.all_to_all(
        outbound,
        ("clus", "trow", "tcol"),
        split_axis=0,
        concat_axis=0,
        tiled=True,
    ).reshape(clusters_count, tile_rows, tile_cols, len(OFFSETS), pair_rows)
    owners = []
    for owner in range(tile_cols):
        candidates = []
        for sender in range(tile_cols):
            j = [(sender + o) % tile_cols for o in OFFSETS].index(owner)
            candidates.append(returned[:, :, sender, j, :])
        owners.append(jnp.max(jnp.stack(candidates), axis=0))
    best = jnp.stack(owners, axis=2).reshape(SLOTS)
    return best[buffer_slot]


def solution(mesh):
    in_specs = (P(("clus", "trow", "tcol"), None), P(("clus", "trow", "tcol")))
    out_specs = P(("clus", "trow", "tcol"))
    return jax.shard_map(
        on_device, mesh=mesh, in_specs=in_specs, out_specs=out_specs, check_vma=False
    )
```

```python
import jax
import jax.numpy as jnp
from jax import lax
from jax.sharding import PartitionSpec as P

CAP = 12288
BLOCK = 768

epsilon = 1e-06
ABSENT = 4.0
OFFSETS = (0, -1, 1, 2)


def shift(x, axis, n, step):
    return lax.ppermute(x, axis, [(i, (i + step) % n) for i in range(n)])


def ring_gather(chunk, axis):
    n = lax.axis_size(axis)
    half = chunk.shape[0] // 2
    from_left = shift(chunk, axis, n, 1)
    from_right = shift(chunk, axis, n, -1)
    far = jnp.concatenate(
        [shift(from_right[:half], axis, n, -1), shift(from_left[half:], axis, n, 1)], axis=0
    )
    return [chunk, from_left, from_right, far]


def block_max(rows, cols, self_block):
    scores = lax.dot_general(
        rows, cols, (((1,), (1,)), ((), ())), preferred_element_type=jnp.float32
    )
    keep = (cols[:, 0].astype(jnp.float32) < 2.0)[None, :]
    if self_block:
        index = jnp.arange(rows.shape[0], dtype=jnp.int32)
        keep = keep & (index[:, None] != index[None, :])
    return jnp.max(jnp.where(keep, scores, -1.0), axis=1)


def on_device(embeddings, target):
    width = embeddings.shape[1]
    clusters_count = lax.axis_size("clus")
    tile_rows = lax.axis_size("trow")
    tile_cols = lax.axis_size("tcol")
    per_cluster = (BLOCK // (clusters_count * tile_rows * tile_cols)) * (CAP // BLOCK)

    values = embeddings.astype(jnp.float32)
    unit_rows = (
        values / jnp.sqrt(jnp.sum(values * values, axis=1, keepdims=True) + epsilon)
    ).astype(jnp.bfloat16)

    cluster = target // CAP
    onehot = (cluster[:, None] == jnp.arange(clusters_count, dtype=jnp.int32)[None, :]).astype(
        jnp.int32
    )
    position = jnp.sum(onehot * (jnp.cumsum(onehot, axis=0) - 1), axis=1)
    outgoing = (
        jnp.full((clusters_count * per_cluster, width), ABSENT, jnp.bfloat16)
        .at[cluster * per_cluster + position]
        .set(unit_rows)
    )
    arrived = lax.all_to_all(
        outgoing.reshape(clusters_count, per_cluster, width),
        "clus",
        split_axis=0,
        concat_axis=0,
        tiled=True,
    ).reshape(clusters_count * per_cluster, width)

    row_chunks = ring_gather(arrived, "tcol")
    col_chunks = ring_gather(arrived, "trow")
    partial = jnp.stack(
        [
            jnp.max(
                jnp.stack(
                    [
                        block_max(rows, cols, a == 0 and b == 0)
                        for b, cols in enumerate(col_chunks)
                    ]
                ),
                axis=0,
            )
            for a, rows in enumerate(row_chunks)
        ]
    )

    col_pos = lax.axis_index("tcol")
    relative = (jnp.arange(tile_cols, dtype=jnp.int32) - col_pos) % tile_cols
    chunk_of = jnp.array(
        [OFFSETS.index(o if o <= tile_cols // 2 else o - tile_cols) for o in range(tile_cols)],
        jnp.int32,
    )
    ordered = partial[chunk_of[relative]]
    outbound = ordered.reshape(tile_cols, clusters_count, per_cluster).transpose(1, 0, 2)
    returned = lax.all_to_all(
        outbound.reshape(clusters_count * tile_cols, per_cluster),
        ("clus", "tcol"),
        split_axis=0,
        concat_axis=0,
        tiled=True,
    ).reshape(clusters_count, tile_cols, per_cluster)
    best = jnp.max(returned, axis=1).reshape(-1)
    return best[cluster * per_cluster + position]


def solution(mesh):
    in_specs = (P(("clus", "trow", "tcol"), None), P(("clus", "trow", "tcol")))
    out_specs = P(("clus", "trow", "tcol"))
    return jax.shard_map(
        on_device, mesh=mesh, in_specs=in_specs, out_specs=out_specs, check_vma=False
    )
```

```python
import jax
import jax.numpy as jnp
from jax import lax
from jax.sharding import PartitionSpec as P

CAP = 12288
BLOCK = 768

epsilon = 1e-06
ABSENT = 4.0
OFFSETS = (0, -1, 1, 2)


def shift(x, axis, n, step):
    return lax.ppermute(x, axis, [(i, (i + step) % n) for i in range(n)])


def ring_gather(chunk, axis):
    n = lax.axis_size(axis)
    half = chunk.shape[0] // 2
    from_left = shift(chunk, axis, n, 1)
    from_right = shift(chunk, axis, n, -1)
    far = jnp.concatenate(
        [shift(from_right[:half], axis, n, -1), shift(from_left[half:], axis, n, 1)], axis=0
    )
    return [chunk, from_left, from_right, far]


def block_max(rows, cols, self_block):
    scores = lax.dot_general(
        rows, cols, (((1,), (1,)), ((), ())), preferred_element_type=jnp.float32
    )
    keep = (cols[:, 0].astype(jnp.float32) < 2.0)[None, :]
    if self_block:
        index = jnp.arange(rows.shape[0], dtype=jnp.int32)
        keep = keep & (index[:, None] != index[None, :])
    return jnp.max(jnp.where(keep, scores, -1.0), axis=1)


def on_device(embeddings, target):
    width = embeddings.shape[1]
    clusters_count = lax.axis_size("clus")
    tile_rows = lax.axis_size("trow")
    tile_cols = lax.axis_size("tcol")
    per_cluster = (BLOCK // (clusters_count * tile_rows * tile_cols)) * (CAP // BLOCK)

    values = embeddings.astype(jnp.float32)
    unit_rows = (
        values / jnp.sqrt(jnp.sum(values * values, axis=1, keepdims=True) + epsilon)
    ).astype(jnp.bfloat16)

    cluster = target // CAP
    onehot = (cluster[:, None] == jnp.arange(clusters_count, dtype=jnp.int32)[None, :]).astype(
        jnp.int32
    )
    position = jnp.sum(onehot * (jnp.cumsum(onehot, axis=0) - 1), axis=1)
    clus_pos = lax.axis_index("clus")
    shift_of = (cluster - clus_pos) % clusters_count
    outgoing = (
        jnp.full((clusters_count * per_cluster, width), ABSENT, jnp.bfloat16)
        .at[shift_of * per_cluster + position]
        .set(unit_rows)
    )
    pieces = [outgoing[:per_cluster]] + [
        shift(outgoing[s * per_cluster : (s + 1) * per_cluster], "clus", clusters_count, s)
        for s in range(1, clusters_count)
    ]
    arrived = jnp.concatenate(pieces, axis=0)

    row_chunks = ring_gather(arrived, "tcol")
    col_chunks = ring_gather(arrived, "trow")
    partial = jnp.stack(
        [
            jnp.max(
                jnp.stack(
                    [
                        block_max(rows, cols, a == 0 and b == 0)
                        for b, cols in enumerate(col_chunks)
                    ]
                ),
                axis=0,
            )
            for a, rows in enumerate(row_chunks)
        ]
    )

    col_pos = lax.axis_index("tcol")
    relative = (jnp.arange(tile_cols, dtype=jnp.int32) - col_pos) % tile_cols
    chunk_of = jnp.array(
        [OFFSETS.index(o if o <= tile_cols // 2 else o - tile_cols) for o in range(tile_cols)],
        jnp.int32,
    )
    ordered = partial[chunk_of[relative]]
    by_shift = ordered.reshape(tile_cols, clusters_count, per_cluster)
    source_shift = (clus_pos - jnp.arange(clusters_count, dtype=jnp.int32)) % clusters_count
    outbound = by_shift[:, source_shift].transpose(1, 0, 2)
    returned = lax.all_to_all(
        outbound.reshape(clusters_count * tile_cols, per_cluster),
        ("clus", "tcol"),
        split_axis=0,
        concat_axis=0,
        tiled=True,
    ).reshape(clusters_count, tile_cols, per_cluster)
    best = jnp.max(returned, axis=1).reshape(-1)
    return best[cluster * per_cluster + position]


def solution(mesh):
    in_specs = (P(("clus", "trow", "tcol"), None), P(("clus", "trow", "tcol")))
    out_specs = P(("clus", "trow", "tcol"))
    return jax.shard_map(
        on_device, mesh=mesh, in_specs=in_specs, out_specs=out_specs, check_vma=False
    )
```

```python
import jax
import jax.numpy as jnp
from jax import lax
from jax.sharding import PartitionSpec as P
from jax.experimental import pallas as pl
from jax.experimental.pallas import tpu as pltpu

CAP = 12288
BLOCK = 768

epsilon = 1e-06
ABSENT = 4.0
OFFSETS = (0, -1, 1, 2)

TILE = 256


def shift(x, axis, n, step):
    return lax.ppermute(x, axis, [(i, (i + step) % n) for i in range(n)])


def ring_gather(chunk, axis):
    n = lax.axis_size(axis)
    half = chunk.shape[0] // 2
    from_left = shift(chunk, axis, n, 1)
    from_right = shift(chunk, axis, n, -1)
    far = jnp.concatenate(
        [shift(from_right[:half], axis, n, -1), shift(from_left[half:], axis, n, 1)], axis=0
    )
    return [chunk, from_left, from_right, far]


def block_kernel(self_block, rows_ref, cols_ref, present_ref, out_ref):
    scores = lax.dot_general(
        rows_ref[...], cols_ref[...], (((1,), (1,)), ((), ())), preferred_element_type=jnp.float32
    )
    keep = present_ref[...] > 0.0
    if self_block:
        row = pl.program_id(0) * TILE + lax.broadcasted_iota(jnp.int32, scores.shape, 0)
        col = lax.broadcasted_iota(jnp.int32, scores.shape, 1)
        keep = keep & (row != col)
    out_ref[...] = jnp.max(jnp.where(keep, scores, -1.0), axis=1, keepdims=True)


def block_max(rows, cols, present, self_block):
    count, width = rows.shape
    columns = cols.shape[0]
    out = pl.pallas_call(
        lambda *refs: block_kernel(self_block, *refs),
        grid=(count // TILE,),
        in_specs=[
            pl.BlockSpec((TILE, width), lambda i: (i, 0)),
            pl.BlockSpec((columns, width), lambda i: (0, 0)),
            pl.BlockSpec((1, columns), lambda i: (0, 0)),
        ],
        out_specs=pl.BlockSpec((TILE, 1), lambda i: (i, 0)),
        out_shape=jax.ShapeDtypeStruct((count, 1), jnp.float32),
    )(rows, cols, present)
    return out.reshape(count)


def on_device(embeddings, target):
    width = embeddings.shape[1]
    clusters_count = lax.axis_size("clus")
    tile_rows = lax.axis_size("trow")
    tile_cols = lax.axis_size("tcol")
    per_cluster = (BLOCK // (clusters_count * tile_rows * tile_cols)) * (CAP // BLOCK)

    values = embeddings.astype(jnp.float32)
    unit_rows = (
        values / jnp.sqrt(jnp.sum(values * values, axis=1, keepdims=True) + epsilon)
    ).astype(jnp.bfloat16)

    cluster = target // CAP
    onehot = (cluster[:, None] == jnp.arange(clusters_count, dtype=jnp.int32)[None, :]).astype(
        jnp.int32
    )
    position = jnp.sum(onehot * (jnp.cumsum(onehot, axis=0) - 1), axis=1)
    outgoing = (
        jnp.full((clusters_count * per_cluster, width), ABSENT, jnp.bfloat16)
        .at[cluster * per_cluster + position]
        .set(unit_rows)
    )
    arrived = lax.all_to_all(
        outgoing.reshape(clusters_count, per_cluster, width),
        "clus",
        split_axis=0,
        concat_axis=0,
        tiled=True,
    ).reshape(clusters_count * per_cluster, width)

    row_chunks = ring_gather(arrived, "tcol")
    col_chunks = ring_gather(arrived, "trow")
    col_present = [
        (cols[:, 0].astype(jnp.float32) < 2.0).astype(jnp.float32)[None, :] for cols in col_chunks
    ]
    partial = jnp.stack(
        [
            jnp.max(
                jnp.stack(
                    [
                        block_max(rows, cols, present, a == 0 and b == 0)
                        for b, (cols, present) in enumerate(zip(col_chunks, col_present))
                    ]
                ),
                axis=0,
            )
            for a, rows in enumerate(row_chunks)
        ]
    )

    col_pos = lax.axis_index("tcol")
    relative = (jnp.arange(tile_cols, dtype=jnp.int32) - col_pos) % tile_cols
    chunk_of = jnp.array(
        [OFFSETS.index(o if o <= tile_cols // 2 else o - tile_cols) for o in range(tile_cols)],
        jnp.int32,
    )
    ordered = partial[chunk_of[relative]]
    outbound = ordered.reshape(tile_cols, clusters_count, per_cluster).transpose(1, 0, 2)
    returned = lax.all_to_all(
        outbound.reshape(clusters_count * tile_cols, per_cluster),
        ("clus", "tcol"),
        split_axis=0,
        concat_axis=0,
        tiled=True,
    ).reshape(clusters_count, tile_cols, per_cluster)
    best = jnp.max(returned, axis=1).reshape(-1)
    return best[cluster * per_cluster + position]


def solution(mesh):
    in_specs = (P(("clus", "trow", "tcol"), None), P(("clus", "trow", "tcol")))
    out_specs = P(("clus", "trow", "tcol"))
    return jax.shard_map(
        on_device, mesh=mesh, in_specs=in_specs, out_specs=out_specs, check_vma=False
    )
```

```python
import jax
import jax.numpy as jnp
from jax import lax
from jax.sharding import PartitionSpec as P

CAP = 12288
BLOCK = 768

epsilon = 1e-06
ABSENT = 4.0
OFFSETS = (0, -1, 1, 2)


def shift(x, axis, n, step):
    return lax.ppermute(x, axis, [(i, (i + step) % n) for i in range(n)])


def ring_gather(chunk, axis):
    n = lax.axis_size(axis)
    half = chunk.shape[0] // 2
    from_left = shift(chunk, axis, n, 1)
    from_right = shift(chunk, axis, n, -1)
    far = jnp.concatenate(
        [shift(from_right[:half], axis, n, -1), shift(from_left[half:], axis, n, 1)], axis=0
    )
    return [chunk, from_left, from_right, far]


def block_max(rows, cols, self_block):
    scores = lax.dot_general(
        rows, cols, (((1,), (1,)), ((), ())), preferred_element_type=jnp.float32
    )
    keep = (cols[:, 0].astype(jnp.float32) < 2.0)[None, :]
    if self_block:
        index = jnp.arange(rows.shape[0], dtype=jnp.int32)
        keep = keep & (index[:, None] != index[None, :])
    return jnp.max(jnp.where(keep, scores, -1.0), axis=1)


def on_device(embeddings, target):
    width = embeddings.shape[1]
    clusters_count = lax.axis_size("clus")
    tile_rows = lax.axis_size("trow")
    tile_cols = lax.axis_size("tcol")
    per_cluster = (BLOCK // (clusters_count * tile_rows * tile_cols)) * (CAP // BLOCK)

    values = embeddings.astype(jnp.float32)
    unit_rows = (
        values / jnp.sqrt(jnp.sum(values * values, axis=1, keepdims=True) + epsilon)
    ).astype(jnp.bfloat16)

    cluster = target // CAP
    onehot = (cluster[:, None] == jnp.arange(clusters_count, dtype=jnp.int32)[None, :]).astype(
        jnp.int32
    )
    position = jnp.sum(onehot * (jnp.cumsum(onehot, axis=0) - 1), axis=1)
    slot = cluster * per_cluster + position
    placed = slot[None, :] == jnp.arange(clusters_count * per_cluster, dtype=jnp.int32)[:, None]
    gathered = jnp.dot(
        placed.astype(jnp.bfloat16), unit_rows, preferred_element_type=jnp.float32
    ).astype(jnp.bfloat16)
    outgoing = jnp.where(jnp.any(placed, axis=1)[:, None], gathered, jnp.bfloat16(ABSENT))
    arrived = lax.all_to_all(
        outgoing.reshape(clusters_count, per_cluster, width),
        "clus",
        split_axis=0,
        concat_axis=0,
        tiled=True,
    ).reshape(clusters_count * per_cluster, width)

    row_chunks = ring_gather(arrived, "tcol")
    col_chunks = ring_gather(arrived, "trow")
    partial = jnp.stack(
        [
            jnp.max(
                jnp.stack(
                    [
                        block_max(rows, cols, a == 0 and b == 0)
                        for b, cols in enumerate(col_chunks)
                    ]
                ),
                axis=0,
            )
            for a, rows in enumerate(row_chunks)
        ]
    )

    col_pos = lax.axis_index("tcol")
    relative = (jnp.arange(tile_cols, dtype=jnp.int32) - col_pos) % tile_cols
    chunk_of = jnp.array(
        [OFFSETS.index(o if o <= tile_cols // 2 else o - tile_cols) for o in range(tile_cols)],
        jnp.int32,
    )
    ordered = partial[chunk_of[relative]]
    outbound = ordered.reshape(tile_cols, clusters_count, per_cluster).transpose(1, 0, 2)
    returned = lax.all_to_all(
        outbound.reshape(clusters_count * tile_cols, per_cluster),
        ("clus", "tcol"),
        split_axis=0,
        concat_axis=0,
        tiled=True,
    ).reshape(clusters_count, tile_cols, per_cluster)
    best = jnp.max(returned, axis=1).reshape(-1)
    return jnp.max(jnp.where(placed.T, best[None, :], -jnp.inf), axis=1)


def solution(mesh):
    in_specs = (P(("clus", "trow", "tcol"), None), P(("clus", "trow", "tcol")))
    out_specs = P(("clus", "trow", "tcol"))
    return jax.shard_map(
        on_device, mesh=mesh, in_specs=in_specs, out_specs=out_specs, check_vma=False
    )
```

```python
import jax
import jax.numpy as jnp
from jax import lax
from jax.sharding import PartitionSpec as P

CAP = 12288
BLOCK = 768

epsilon = 1e-06
ABSENT = 4.0
OFFSETS = (0, -1, 1, 2)


def shift(x, axis, n, step):
    return lax.ppermute(x, axis, [(i, (i + step) % n) for i in range(n)])


def ring_gather(chunk, axis):
    n = lax.axis_size(axis)
    half = chunk.shape[0] // 2
    from_left = shift(chunk, axis, n, 1)
    from_right = shift(chunk, axis, n, -1)
    far = jnp.concatenate(
        [shift(from_right[:half], axis, n, -1), shift(from_left[half:], axis, n, 1)], axis=0
    )
    return [chunk, from_left, from_right, far]


def block_max(rows, cols, self_block):
    half = rows.shape[0] // 2
    keep = (cols[:, 0].astype(jnp.float32) < 2.0)[None, :]
    out = []
    for h in range(2):
        scores = lax.dot_general(
            rows[h * half : (h + 1) * half], cols, (((1,), (1,)), ((), ())),
            preferred_element_type=jnp.float32,
        )
        k = keep
        if self_block:
            index = jnp.arange(rows.shape[0], dtype=jnp.int32)
            k = keep & (index[h * half : (h + 1) * half, None] != index[None, :])
        out.append(jnp.max(jnp.where(k, scores, -1.0), axis=1))
    return jnp.concatenate(out)


def on_device(embeddings, target):
    width = embeddings.shape[1]
    clusters_count = lax.axis_size("clus")
    tile_rows = lax.axis_size("trow")
    tile_cols = lax.axis_size("tcol")
    per_cluster = (BLOCK // (clusters_count * tile_rows * tile_cols)) * (CAP // BLOCK)

    values = embeddings.astype(jnp.float32)
    unit_rows = (
        values / jnp.sqrt(jnp.sum(values * values, axis=1, keepdims=True) + epsilon)
    ).astype(jnp.bfloat16)

    cluster = target // CAP
    onehot = (cluster[:, None] == jnp.arange(clusters_count, dtype=jnp.int32)[None, :]).astype(
        jnp.int32
    )
    position = jnp.sum(onehot * (jnp.cumsum(onehot, axis=0) - 1), axis=1)
    slot = cluster * per_cluster + position
    placed = slot[None, :] == jnp.arange(clusters_count * per_cluster, dtype=jnp.int32)[:, None]
    gathered = jnp.dot(
        placed.astype(jnp.bfloat16), unit_rows, preferred_element_type=jnp.float32
    ).astype(jnp.bfloat16)
    outgoing = jnp.where(jnp.any(placed, axis=1)[:, None], gathered, jnp.bfloat16(ABSENT))
    arrived = lax.all_to_all(
        outgoing.reshape(clusters_count, per_cluster, width),
        "clus",
        split_axis=0,
        concat_axis=0,
        tiled=True,
    ).reshape(clusters_count * per_cluster, width)

    row_chunks = ring_gather(arrived, "tcol")
    col_chunks = ring_gather(arrived, "trow")
    partial = jnp.stack(
        [
            jnp.max(
                jnp.stack(
                    [
                        block_max(rows, cols, a == 0 and b == 0)
                        for b, cols in enumerate(col_chunks)
                    ]
                ),
                axis=0,
            )
            for a, rows in enumerate(row_chunks)
        ]
    )

    col_pos = lax.axis_index("tcol")
    relative = (jnp.arange(tile_cols, dtype=jnp.int32) - col_pos) % tile_cols
    chunk_of = jnp.array(
        [OFFSETS.index(o if o <= tile_cols // 2 else o - tile_cols) for o in range(tile_cols)],
        jnp.int32,
    )
    ordered = partial[chunk_of[relative]]
    outbound = ordered.reshape(tile_cols, clusters_count, per_cluster).transpose(1, 0, 2)
    returned = lax.all_to_all(
        outbound.reshape(clusters_count * tile_cols, per_cluster),
        ("clus", "tcol"),
        split_axis=0,
        concat_axis=0,
        tiled=True,
    ).reshape(clusters_count, tile_cols, per_cluster)
    best = jnp.max(returned, axis=1).reshape(-1)
    return jnp.max(jnp.where(placed.T, best[None, :], -jnp.inf), axis=1)


def solution(mesh):
    in_specs = (P(("clus", "trow", "tcol"), None), P(("clus", "trow", "tcol")))
    out_specs = P(("clus", "trow", "tcol"))
    return jax.shard_map(
        on_device, mesh=mesh, in_specs=in_specs, out_specs=out_specs, check_vma=False
    )
```

```python
import jax
import jax.numpy as jnp
from jax import lax
from jax.sharding import PartitionSpec as P

CAP = 12288
BLOCK = 768

epsilon = 1e-06
ABSENT = 4.0
OFFSETS = (0, -1, 1, 2)


def shift(x, axis, n, step):
    return lax.ppermute(x, axis, [(i, (i + step) % n) for i in range(n)])


def ring_halves(chunk, axis):
    n = lax.axis_size(axis)
    half = chunk.shape[0] // 2
    first, second = chunk[:half], chunk[half:]
    right_first = shift(first, axis, n, -1)
    left_second = shift(second, axis, n, 1)
    right_second = shift(second, axis, n, -1)
    left_first = shift(first, axis, n, 1)
    far_first = shift(right_first, axis, n, -1)
    far_second = shift(left_second, axis, n, 1)
    return [
        (first, second),
        (left_first, left_second),
        (right_first, right_second),
        (far_first, far_second),
    ]


def block_max(rows, cols, self_block):
    half = rows.shape[0] // 2
    keep = (cols[:, 0].astype(jnp.float32) < 2.0)[None, :]
    out = []
    for h in range(2):
        scores = lax.dot_general(
            rows[h * half : (h + 1) * half], cols, (((1,), (1,)), ((), ())),
            preferred_element_type=jnp.float32,
        )
        k = keep
        if self_block:
            index = jnp.arange(rows.shape[0], dtype=jnp.int32)
            k = keep & (index[h * half : (h + 1) * half, None] != index[None, :])
        out.append(jnp.max(jnp.where(k, scores, -1.0), axis=1))
    return jnp.concatenate(out)


def on_device(embeddings, target):
    width = embeddings.shape[1]
    clusters_count = lax.axis_size("clus")
    tile_rows = lax.axis_size("trow")
    tile_cols = lax.axis_size("tcol")
    per_cluster = (BLOCK // (clusters_count * tile_rows * tile_cols)) * (CAP // BLOCK)

    values = embeddings.astype(jnp.float32)
    unit_rows = (
        values / jnp.sqrt(jnp.sum(values * values, axis=1, keepdims=True) + epsilon)
    ).astype(jnp.bfloat16)

    cluster = target // CAP
    onehot = (cluster[:, None] == jnp.arange(clusters_count, dtype=jnp.int32)[None, :]).astype(
        jnp.int32
    )
    position = jnp.sum(onehot * (jnp.cumsum(onehot, axis=0) - 1), axis=1)
    slot = cluster * per_cluster + position
    placed = slot[None, :] == jnp.arange(clusters_count * per_cluster, dtype=jnp.int32)[:, None]
    gathered = jnp.dot(
        placed.astype(jnp.bfloat16), unit_rows, preferred_element_type=jnp.float32
    ).astype(jnp.bfloat16)
    outgoing = jnp.where(jnp.any(placed, axis=1)[:, None], gathered, jnp.bfloat16(ABSENT))
    arrived = lax.all_to_all(
        outgoing.reshape(clusters_count, per_cluster, width),
        "clus",
        split_axis=0,
        concat_axis=0,
        tiled=True,
    ).reshape(clusters_count * per_cluster, width)

    row_chunks = [jnp.concatenate(h, axis=0) for h in ring_halves(arrived, "tcol")]
    col_chunks = [arrived] + [
        jnp.concatenate(h, axis=0) for h in ring_halves(arrived, "trow")[1:]
    ]
    partial = jnp.stack(
        [
            jnp.max(
                jnp.stack(
                    [
                        block_max(rows, cols, a == 0 and b == 0)
                        for b, cols in enumerate(col_chunks)
                    ]
                ),
                axis=0,
            )
            for a, rows in enumerate(row_chunks)
        ]
    )

    col_pos = lax.axis_index("tcol")
    relative = (jnp.arange(tile_cols, dtype=jnp.int32) - col_pos) % tile_cols
    chunk_of = jnp.array(
        [OFFSETS.index(o if o <= tile_cols // 2 else o - tile_cols) for o in range(tile_cols)],
        jnp.int32,
    )
    ordered = partial[chunk_of[relative]]
    outbound = ordered.reshape(tile_cols, clusters_count, per_cluster).transpose(1, 0, 2)
    returned = lax.all_to_all(
        outbound.reshape(clusters_count * tile_cols, per_cluster),
        ("clus", "tcol"),
        split_axis=0,
        concat_axis=0,
        tiled=True,
    ).reshape(clusters_count, tile_cols, per_cluster)
    best = jnp.max(returned, axis=1).reshape(-1)
    return jnp.max(jnp.where(placed.T, best[None, :], -jnp.inf), axis=1)


def solution(mesh):
    in_specs = (P(("clus", "trow", "tcol"), None), P(("clus", "trow", "tcol")))
    out_specs = P(("clus", "trow", "tcol"))
    return jax.shard_map(
        on_device, mesh=mesh, in_specs=in_specs, out_specs=out_specs, check_vma=False
    )
```

```python
import jax
import jax.numpy as jnp
from jax import lax
from jax.sharding import PartitionSpec as P

CAP = 12288
BLOCK = 768

epsilon = 1e-06
ABSENT = 4.0
OFFSETS = (0, -1, 1, 2)


def shift(x, axis, n, step):
    return lax.ppermute(x, axis, [(i, (i + step) % n) for i in range(n)])


def ring_gather(chunk, axis):
    n = lax.axis_size(axis)
    half = chunk.shape[0] // 2
    from_left = shift(chunk, axis, n, 1)
    from_right = shift(chunk, axis, n, -1)
    far = jnp.concatenate(
        [shift(from_right[:half], axis, n, -1), shift(from_left[half:], axis, n, 1)], axis=0
    )
    return [chunk, from_left, from_right, far]


def block_max(rows, cols, self_block):
    half = rows.shape[0] // 2
    keep = (cols[:, 0].astype(jnp.float32) < 2.0)[None, :]
    out = []
    for h in range(2):
        scores = lax.dot_general(
            rows[h * half : (h + 1) * half], cols, (((1,), (1,)), ((), ())),
            preferred_element_type=jnp.float32,
        )
        k = keep
        if self_block:
            index = jnp.arange(rows.shape[0], dtype=jnp.int32)
            k = keep & (index[h * half : (h + 1) * half, None] != index[None, :])
        out.append(jnp.max(jnp.where(k, scores, -1.0), axis=1))
    return jnp.concatenate(out)


def on_device(embeddings, target):
    width = embeddings.shape[1]
    clusters_count = lax.axis_size("clus")
    tile_rows = lax.axis_size("trow")
    tile_cols = lax.axis_size("tcol")
    per_cluster = (BLOCK // (clusters_count * tile_rows * tile_cols)) * (CAP // BLOCK)

    values = embeddings.astype(jnp.float32)
    unit_rows = (
        values / jnp.sqrt(jnp.sum(values * values, axis=1, keepdims=True) + epsilon)
    ).astype(jnp.bfloat16)

    cluster = target // CAP
    onehot = (cluster[:, None] == jnp.arange(clusters_count, dtype=jnp.int32)[None, :]).astype(
        jnp.int32
    )
    count = onehot.shape[0]
    earlier = (
        jnp.arange(count, dtype=jnp.int32)[None, :] < jnp.arange(count, dtype=jnp.int32)[:, None]
    ).astype(jnp.bfloat16)
    before = jnp.dot(earlier, onehot.astype(jnp.bfloat16), preferred_element_type=jnp.float32)
    position = jnp.sum(onehot * before.astype(jnp.int32), axis=1)
    slot = cluster * per_cluster + position
    placed = slot[None, :] == jnp.arange(clusters_count * per_cluster, dtype=jnp.int32)[:, None]
    gathered = jnp.dot(
        placed.astype(jnp.bfloat16), unit_rows, preferred_element_type=jnp.float32
    ).astype(jnp.bfloat16)
    outgoing = jnp.where(jnp.any(placed, axis=1)[:, None], gathered, jnp.bfloat16(ABSENT))
    arrived = lax.all_to_all(
        outgoing.reshape(clusters_count, per_cluster, width),
        "clus",
        split_axis=0,
        concat_axis=0,
        tiled=True,
    ).reshape(clusters_count * per_cluster, width)

    row_chunks = ring_gather(arrived, "tcol")
    col_chunks = ring_gather(arrived, "trow")
    partial = jnp.stack(
        [
            jnp.max(
                jnp.stack(
                    [
                        block_max(rows, cols, a == 0 and b == 0)
                        for b, cols in enumerate(col_chunks)
                    ]
                ),
                axis=0,
            )
            for a, rows in enumerate(row_chunks)
        ]
    )

    col_pos = lax.axis_index("tcol")
    relative = (jnp.arange(tile_cols, dtype=jnp.int32) - col_pos) % tile_cols
    chunk_of = jnp.array(
        [OFFSETS.index(o if o <= tile_cols // 2 else o - tile_cols) for o in range(tile_cols)],
        jnp.int32,
    )
    ordered = partial[chunk_of[relative]]
    outbound = ordered.reshape(tile_cols, clusters_count, per_cluster).transpose(1, 0, 2)
    returned = lax.all_to_all(
        outbound.reshape(clusters_count * tile_cols, per_cluster),
        ("clus", "tcol"),
        split_axis=0,
        concat_axis=0,
        tiled=True,
    ).reshape(clusters_count, tile_cols, per_cluster)
    best = jnp.max(returned, axis=1).reshape(-1)
    return jnp.max(jnp.where(placed.T, best[None, :], -jnp.inf), axis=1)


def solution(mesh):
    in_specs = (P(("clus", "trow", "tcol"), None), P(("clus", "trow", "tcol")))
    out_specs = P(("clus", "trow", "tcol"))
    return jax.shard_map(
        on_device, mesh=mesh, in_specs=in_specs, out_specs=out_specs, check_vma=False
    )
```

```python
import jax
import jax.numpy as jnp
from jax import lax
from jax.sharding import PartitionSpec as P

CAP = 12288
BLOCK = 768

epsilon = 1e-06
ABSENT = 4.0
OFFSETS = (0, -1, 1, 2)


def shift(x, axis, n, step):
    return lax.ppermute(x, axis, [(i, (i + step) % n) for i in range(n)])


def ring_gather(chunk, axis):
    n = lax.axis_size(axis)
    half = chunk.shape[0] // 2
    from_left = shift(chunk, axis, n, 1)
    from_right = shift(chunk, axis, n, -1)
    far = jnp.concatenate(
        [shift(from_right[:half], axis, n, -1), shift(from_left[half:], axis, n, 1)], axis=0
    )
    return [chunk, from_left, from_right, far]


def block_max(rows, cols, self_block):
    half = rows.shape[0] // 2
    keep = (cols[:, 0].astype(jnp.float32) < 2.0)[None, :]
    out = []
    for h in range(2):
        scores = lax.dot_general(
            rows[h * half : (h + 1) * half], cols, (((1,), (1,)), ((), ())),
            preferred_element_type=jnp.float32,
        )
        k = keep
        if self_block:
            index = jnp.arange(rows.shape[0], dtype=jnp.int32)
            k = keep & (index[h * half : (h + 1) * half, None] != index[None, :])
        out.append(jnp.max(jnp.where(k, scores, -1.0), axis=1))
    return jnp.concatenate(out)


def on_device(embeddings, target):
    width = embeddings.shape[1]
    clusters_count = lax.axis_size("clus")
    tile_rows = lax.axis_size("trow")
    tile_cols = lax.axis_size("tcol")
    per_cluster = (BLOCK // (clusters_count * tile_rows * tile_cols)) * (CAP // BLOCK)

    values = embeddings.astype(jnp.float32)
    unit_rows = (
        values / jnp.sqrt(jnp.sum(values * values, axis=1, keepdims=True) + epsilon)
    ).astype(jnp.bfloat16)

    cluster = target // CAP
    onehot = (cluster[:, None] == jnp.arange(clusters_count, dtype=jnp.int32)[None, :]).astype(
        jnp.int32
    )
    count = onehot.shape[0]
    earlier = (
        jnp.arange(count, dtype=jnp.int32)[None, :] < jnp.arange(count, dtype=jnp.int32)[:, None]
    ).astype(jnp.bfloat16)
    before = jnp.dot(earlier, onehot.astype(jnp.bfloat16), preferred_element_type=jnp.float32)
    position = jnp.sum(onehot * before.astype(jnp.int32), axis=1)
    slot = cluster * per_cluster + position
    placed = slot[None, :] == jnp.arange(clusters_count * per_cluster, dtype=jnp.int32)[:, None]
    gathered = jnp.dot(
        placed.astype(jnp.bfloat16), unit_rows, preferred_element_type=jnp.float32
    ).astype(jnp.bfloat16)
    outgoing = jnp.where(jnp.any(placed, axis=1)[:, None], gathered, jnp.bfloat16(ABSENT))
    arrived = lax.all_to_all(
        outgoing.reshape(clusters_count, per_cluster, width),
        "clus",
        split_axis=0,
        concat_axis=0,
        tiled=True,
    ).reshape(clusters_count * per_cluster, width)

    row_chunks = ring_gather(arrived, "tcol")
    col_chunks = ring_gather(arrived, "trow")
    partial = jnp.stack(
        [
            jnp.max(
                jnp.stack(
                    [
                        block_max(rows, cols, a == 0 and b == 0)
                        for b, cols in enumerate(col_chunks)
                    ]
                ),
                axis=0,
            )
            for a, rows in enumerate(row_chunks)
        ]
    )

    own_best = jnp.max(
        jnp.stack(
            [partial[0]]
            + [
                shift(partial[j], "tcol", tile_cols, OFFSETS[j])
                for j in range(1, len(OFFSETS))
            ]
        ),
        axis=0,
    )
    best = lax.all_to_all(
        own_best.reshape(clusters_count, per_cluster),
        "clus",
        split_axis=0,
        concat_axis=0,
        tiled=True,
    ).reshape(-1)
    return jnp.max(jnp.where(placed.T, best[None, :], -jnp.inf), axis=1)


def solution(mesh):
    in_specs = (P(("clus", "trow", "tcol"), None), P(("clus", "trow", "tcol")))
    out_specs = P(("clus", "trow", "tcol"))
    return jax.shard_map(
        on_device, mesh=mesh, in_specs=in_specs, out_specs=out_specs, check_vma=False
    )
```

```python
import jax
import jax.numpy as jnp
from jax import lax
from jax.sharding import PartitionSpec as P

CAP = 12288
BLOCK = 768

epsilon = 1e-06
ABSENT = 4.0
OFFSETS = (0, -1, 1, 2)


def shift(x, axis, n, step):
    return lax.ppermute(x, axis, [(i, (i + step) % n) for i in range(n)])


def ring_gather(chunk, axis):
    n = lax.axis_size(axis)
    half = chunk.shape[0] // 2
    from_left = shift(chunk, axis, n, 1)
    from_right = shift(chunk, axis, n, -1)
    far = jnp.concatenate(
        [shift(from_right[:half], axis, n, -1), shift(from_left[half:], axis, n, 1)], axis=0
    )
    return [chunk, from_left, from_right, far]


def block_max(rows, cols, self_block):
    scores = lax.dot_general(
        rows, cols, (((1,), (1,)), ((), ())), preferred_element_type=jnp.float32
    )
    keep = (cols[:, 0].astype(jnp.float32) < 2.0)[None, :]
    if self_block:
        index = jnp.arange(rows.shape[0], dtype=jnp.int32)
        keep = keep & (index[:, None] != index[None, :])
    return jnp.max(jnp.where(keep, scores, -1.0), axis=1)


def on_device(embeddings, target):
    width = embeddings.shape[1]
    clusters_count = lax.axis_size("clus")
    tile_rows = lax.axis_size("trow")
    tile_cols = lax.axis_size("tcol")
    per_cluster = (BLOCK // (clusters_count * tile_rows * tile_cols)) * (CAP // BLOCK)

    values = embeddings.astype(jnp.float32)
    unit_rows = (
        values / jnp.sqrt(jnp.sum(values * values, axis=1, keepdims=True) + epsilon)
    ).astype(jnp.bfloat16)

    cluster = target // CAP
    onehot = (cluster[:, None] == jnp.arange(clusters_count, dtype=jnp.int32)[None, :]).astype(
        jnp.int32
    )
    count = onehot.shape[0]
    earlier = (
        jnp.arange(count, dtype=jnp.int32)[None, :] < jnp.arange(count, dtype=jnp.int32)[:, None]
    ).astype(jnp.bfloat16)
    before = jnp.dot(earlier, onehot.astype(jnp.bfloat16), preferred_element_type=jnp.float32)
    position = jnp.sum(onehot * before.astype(jnp.int32), axis=1)
    slot = cluster * per_cluster + position
    placed = slot[None, :] == jnp.arange(clusters_count * per_cluster, dtype=jnp.int32)[:, None]
    gathered = jnp.dot(
        placed.astype(jnp.bfloat16), unit_rows, preferred_element_type=jnp.float32
    ).astype(jnp.bfloat16)
    outgoing = jnp.where(jnp.any(placed, axis=1)[:, None], gathered, jnp.bfloat16(ABSENT))
    arrived = lax.all_to_all(
        outgoing.reshape(clusters_count, per_cluster, width),
        "clus",
        split_axis=0,
        concat_axis=0,
        tiled=True,
    ).reshape(clusters_count * per_cluster, width)

    row_chunks = ring_gather(arrived, "tcol")
    col_chunks = ring_gather(arrived, "trow")
    partial = jnp.stack(
        [
            jnp.max(
                jnp.stack(
                    [
                        block_max(rows, cols, a == 0 and b == 0)
                        for b, cols in enumerate(col_chunks)
                    ]
                ),
                axis=0,
            )
            for a, rows in enumerate(row_chunks)
        ]
    )

    own_best = jnp.max(
        jnp.stack(
            [partial[0]]
            + [
                shift(partial[j], "tcol", tile_cols, OFFSETS[j])
                for j in range(1, len(OFFSETS))
            ]
        ),
        axis=0,
    )
    best = lax.all_to_all(
        own_best.reshape(clusters_count, per_cluster),
        "clus",
        split_axis=0,
        concat_axis=0,
        tiled=True,
    ).reshape(-1)
    return jnp.max(jnp.where(placed.T, best[None, :], -jnp.inf), axis=1)


def solution(mesh):
    in_specs = (P(("clus", "trow", "tcol"), None), P(("clus", "trow", "tcol")))
    out_specs = P(("clus", "trow", "tcol"))
    return jax.shard_map(
        on_device, mesh=mesh, in_specs=in_specs, out_specs=out_specs, check_vma=False
    )
```

```python
import jax
import jax.numpy as jnp
from jax import lax
from jax.sharding import PartitionSpec as P

CAP = 12288
BLOCK = 768

epsilon = 1e-06
ABSENT = 4.0
OFFSETS = (0, -1, 1, 2)


def shift(x, axis, n, step):
    return lax.ppermute(x, axis, [(i, (i + step) % n) for i in range(n)])


def ring_gather(chunk, axis):
    n = lax.axis_size(axis)
    half = chunk.shape[0] // 2
    from_left = shift(chunk, axis, n, 1)
    from_right = shift(chunk, axis, n, -1)
    far = jnp.concatenate(
        [shift(from_right[:half], axis, n, -1), shift(from_left[half:], axis, n, 1)], axis=0
    )
    return [chunk, from_left, from_right, far]


def block_max(rows, cols, self_block):
    scores = lax.dot_general(
        rows, cols, (((1,), (1,)), ((), ())), preferred_element_type=jnp.float32
    )
    keep = (cols[:, 0].astype(jnp.float32) < 2.0)[None, :]
    if self_block:
        index = jnp.arange(rows.shape[0], dtype=jnp.int32)
        keep = keep & (index[:, None] != index[None, :])
    return jnp.max(jnp.where(keep, scores, -1.0), axis=1)


def on_device(embeddings, target):
    width = embeddings.shape[1]
    clusters_count = lax.axis_size("clus")
    tile_rows = lax.axis_size("trow")
    tile_cols = lax.axis_size("tcol")
    per_cluster = (BLOCK // (clusters_count * tile_rows * tile_cols)) * (CAP // BLOCK)

    values = embeddings.astype(jnp.float32)
    unit_rows = (
        values / jnp.sqrt(jnp.sum(values * values, axis=1, keepdims=True) + epsilon)
    ).astype(jnp.bfloat16)

    cluster = target // CAP
    onehot = (cluster[:, None] == jnp.arange(clusters_count, dtype=jnp.int32)[None, :]).astype(
        jnp.int32
    )
    count = onehot.shape[0]
    earlier = (
        jnp.arange(count, dtype=jnp.int32)[None, :] < jnp.arange(count, dtype=jnp.int32)[:, None]
    ).astype(jnp.bfloat16)
    before = jnp.dot(earlier, onehot.astype(jnp.bfloat16), preferred_element_type=jnp.float32)
    position = jnp.sum(onehot * before.astype(jnp.int32), axis=1)
    clus_pos = lax.axis_index("clus")
    slot = ((cluster - clus_pos) % clusters_count) * per_cluster + position
    placed = slot[None, :] == jnp.arange(clusters_count * per_cluster, dtype=jnp.int32)[:, None]
    gathered = jnp.dot(
        placed.astype(jnp.bfloat16), unit_rows, preferred_element_type=jnp.float32
    ).astype(jnp.bfloat16)
    outgoing = jnp.where(jnp.any(placed, axis=1)[:, None], gathered, jnp.bfloat16(ABSENT))
    pieces = [outgoing[:per_cluster]] + [
        shift(outgoing[s * per_cluster : (s + 1) * per_cluster], "clus", clusters_count, s)
        for s in range(1, clusters_count)
    ]
    arrived = jnp.concatenate(pieces, axis=0)

    row_chunks = ring_gather(arrived, "tcol")
    col_chunks = ring_gather(arrived, "trow")
    partial = jnp.stack(
        [
            jnp.max(
                jnp.stack(
                    [
                        block_max(rows, cols, a == 0 and b == 0)
                        for b, cols in enumerate(col_chunks)
                    ]
                ),
                axis=0,
            )
            for a, rows in enumerate(row_chunks)
        ]
    )

    own_best = jnp.max(
        jnp.stack(
            [partial[0]]
            + [
                shift(partial[j], "tcol", tile_cols, OFFSETS[j])
                for j in range(1, len(OFFSETS))
            ]
        ),
        axis=0,
    )
    source_shift = (clus_pos - jnp.arange(clusters_count, dtype=jnp.int32)) % clusters_count
    best = lax.all_to_all(
        own_best.reshape(clusters_count, per_cluster)[source_shift],
        "clus",
        split_axis=0,
        concat_axis=0,
        tiled=True,
    ).reshape(-1)
    own_slot = cluster * per_cluster + position
    owned = own_slot[:, None] == jnp.arange(clusters_count * per_cluster, dtype=jnp.int32)[None, :]
    return jnp.max(jnp.where(owned, best[None, :], -jnp.inf), axis=1)


def solution(mesh):
    in_specs = (P(("clus", "trow", "tcol"), None), P(("clus", "trow", "tcol")))
    out_specs = P(("clus", "trow", "tcol"))
    return jax.shard_map(
        on_device, mesh=mesh, in_specs=in_specs, out_specs=out_specs, check_vma=False
    )
```

```python
import jax
import jax.numpy as jnp
from jax import lax
from jax.sharding import PartitionSpec as P

CAP = 12288
BLOCK = 768

epsilon = 1e-06
ABSENT = 4.0
OFFSETS = (0, -1, 1, 2)


def shift(x, axis, n, step):
    return lax.ppermute(x, axis, [(i, (i + step) % n) for i in range(n)])


def ring_gather(chunk, axis):
    n = lax.axis_size(axis)
    half = chunk.shape[0] // 2
    first, second = chunk[:half], chunk[half:]
    right_first = shift(first, axis, n, -1)
    left_second = shift(second, axis, n, 1)
    first, second, right_first, left_second = lax.optimization_barrier(
        (first, second, right_first, left_second)
    )
    right_second = shift(second, axis, n, -1)
    left_first = shift(first, axis, n, 1)
    far_first = shift(right_first, axis, n, -1)
    far_second = shift(left_second, axis, n, 1)
    return [
        chunk,
        jnp.concatenate([left_first, left_second], axis=0),
        jnp.concatenate([right_first, right_second], axis=0),
        jnp.concatenate([far_first, far_second], axis=0),
    ]


def block_max(rows, cols, self_block):
    scores = lax.dot_general(
        rows, cols, (((1,), (1,)), ((), ())), preferred_element_type=jnp.float32
    )
    keep = (cols[:, 0].astype(jnp.float32) < 2.0)[None, :]
    if self_block:
        index = jnp.arange(rows.shape[0], dtype=jnp.int32)
        keep = keep & (index[:, None] != index[None, :])
    return jnp.max(jnp.where(keep, scores, -1.0), axis=1)


def on_device(embeddings, target):
    width = embeddings.shape[1]
    clusters_count = lax.axis_size("clus")
    tile_rows = lax.axis_size("trow")
    tile_cols = lax.axis_size("tcol")
    per_cluster = (BLOCK // (clusters_count * tile_rows * tile_cols)) * (CAP // BLOCK)

    values = embeddings.astype(jnp.float32)
    unit_rows = (
        values / jnp.sqrt(jnp.sum(values * values, axis=1, keepdims=True) + epsilon)
    ).astype(jnp.bfloat16)

    cluster = target // CAP
    onehot = (cluster[:, None] == jnp.arange(clusters_count, dtype=jnp.int32)[None, :]).astype(
        jnp.int32
    )
    count = onehot.shape[0]
    earlier = (
        jnp.arange(count, dtype=jnp.int32)[None, :] < jnp.arange(count, dtype=jnp.int32)[:, None]
    ).astype(jnp.bfloat16)
    before = jnp.dot(earlier, onehot.astype(jnp.bfloat16), preferred_element_type=jnp.float32)
    position = jnp.sum(onehot * before.astype(jnp.int32), axis=1)
    slot = cluster * per_cluster + position
    placed = slot[None, :] == jnp.arange(clusters_count * per_cluster, dtype=jnp.int32)[:, None]
    gathered = jnp.dot(
        placed.astype(jnp.bfloat16), unit_rows, preferred_element_type=jnp.float32
    ).astype(jnp.bfloat16)
    outgoing = jnp.where(jnp.any(placed, axis=1)[:, None], gathered, jnp.bfloat16(ABSENT))
    arrived = lax.all_to_all(
        outgoing.reshape(clusters_count, per_cluster, width),
        "clus",
        split_axis=0,
        concat_axis=0,
        tiled=True,
    ).reshape(clusters_count * per_cluster, width)

    row_chunks = ring_gather(arrived, "tcol")
    col_chunks = ring_gather(arrived, "trow")
    partial = jnp.stack(
        [
            jnp.max(
                jnp.stack(
                    [
                        block_max(rows, cols, a == 0 and b == 0)
                        for b, cols in enumerate(col_chunks)
                    ]
                ),
                axis=0,
            )
            for a, rows in enumerate(row_chunks)
        ]
    )

    own_best = jnp.max(
        jnp.stack(
            [partial[0]]
            + [
                shift(partial[j], "tcol", tile_cols, OFFSETS[j])
                for j in range(1, len(OFFSETS))
            ]
        ),
        axis=0,
    )
    best = lax.all_to_all(
        own_best.reshape(clusters_count, per_cluster),
        "clus",
        split_axis=0,
        concat_axis=0,
        tiled=True,
    ).reshape(-1)
    return jnp.max(jnp.where(placed.T, best[None, :], -jnp.inf), axis=1)


def solution(mesh):
    in_specs = (P(("clus", "trow", "tcol"), None), P(("clus", "trow", "tcol")))
    out_specs = P(("clus", "trow", "tcol"))
    return jax.shard_map(
        on_device, mesh=mesh, in_specs=in_specs, out_specs=out_specs, check_vma=False
    )
```

```python
import jax
import jax.numpy as jnp
from jax import lax
from jax.sharding import PartitionSpec as P

CAP = 12288
BLOCK = 768

epsilon = 1e-06
ABSENT = 4.0
OFFSETS = (0, -1, 1, 2)


def shift(x, axis, n, step):
    return lax.ppermute(x, axis, [(i, (i + step) % n) for i in range(n)])


def ring_gather(chunk, axis):
    n = lax.axis_size(axis)
    half = chunk.shape[0] // 2
    from_left = shift(chunk, axis, n, 1)
    from_right = shift(chunk, axis, n, -1)
    far = jnp.concatenate(
        [shift(from_right[:half], axis, n, -1), shift(from_left[half:], axis, n, 1)], axis=0
    )
    return [chunk, from_left, from_right, far]


def block_max(rows, cols, self_block):
    scores = lax.dot_general(
        rows, cols, (((1,), (1,)), ((), ())), preferred_element_type=jnp.float32
    )
    keep = (cols[:, 0].astype(jnp.float32) < 2.0)[None, :]
    if self_block:
        index = jnp.arange(rows.shape[0], dtype=jnp.int32)
        keep = keep & (index[:, None] != index[None, :])
    return jnp.max(jnp.where(keep, scores, -1.0), axis=1)


def on_device(embeddings, target):
    width = embeddings.shape[1]
    clusters_count = lax.axis_size("clus")
    tile_rows = lax.axis_size("trow")
    tile_cols = lax.axis_size("tcol")
    per_cluster = (BLOCK // (clusters_count * tile_rows * tile_cols)) * (CAP // BLOCK)

    values = embeddings.astype(jnp.float32)
    unit_rows = (
        values / jnp.sqrt(jnp.sum(values * values, axis=1, keepdims=True) + epsilon)
    ).astype(jnp.bfloat16)

    cluster = target // CAP
    onehot = (cluster[:, None] == jnp.arange(clusters_count, dtype=jnp.int32)[None, :]).astype(
        jnp.int32
    )
    count = onehot.shape[0]
    earlier = (
        jnp.arange(count, dtype=jnp.int32)[None, :] < jnp.arange(count, dtype=jnp.int32)[:, None]
    ).astype(jnp.bfloat16)
    before = jnp.dot(earlier, onehot.astype(jnp.bfloat16), preferred_element_type=jnp.float32)
    position = jnp.sum(onehot * before.astype(jnp.int32), axis=1)
    slot = cluster * per_cluster + position
    placed = slot[None, :] == jnp.arange(clusters_count * per_cluster, dtype=jnp.int32)[:, None]
    gathered = jnp.dot(
        placed.astype(jnp.bfloat16), unit_rows, preferred_element_type=jnp.float32
    ).astype(jnp.bfloat16)
    outgoing = jnp.where(jnp.any(placed, axis=1)[:, None], gathered, jnp.bfloat16(ABSENT))
    arrived = lax.all_to_all(
        outgoing.reshape(clusters_count, per_cluster, width),
        "clus",
        split_axis=0,
        concat_axis=0,
        tiled=True,
    ).reshape(clusters_count * per_cluster, width)

    row_chunks = ring_gather(arrived, "tcol")
    col_chunks = ring_gather(arrived, "trow")
    partial = jnp.stack(
        [
            jnp.max(
                jnp.stack(
                    [
                        block_max(rows, cols, a == 0 and b == 0)
                        for b, cols in enumerate(col_chunks)
                    ]
                ),
                axis=0,
            )
            for a, rows in enumerate(row_chunks)
        ]
    )

    own_best = jnp.max(
        jnp.stack(
            [partial[0]]
            + [
                shift(partial[j], "tcol", tile_cols, OFFSETS[j])
                for j in range(1, len(OFFSETS))
            ]
        ),
        axis=0,
    )
    best = lax.all_to_all(
        own_best.reshape(clusters_count, per_cluster),
        "clus",
        split_axis=0,
        concat_axis=0,
        tiled=True,
    )
    owned = (cluster[:, None, None] == jnp.arange(clusters_count)[None, :, None]) & (
        position[:, None, None] == jnp.arange(per_cluster)[None, None, :]
    )
    return jnp.max(jnp.where(owned, best[None], -jnp.inf), axis=(1, 2))


def solution(mesh):
    in_specs = (P(("clus", "trow", "tcol"), None), P(("clus", "trow", "tcol")))
    out_specs = P(("clus", "trow", "tcol"))
    return jax.shard_map(
        on_device, mesh=mesh, in_specs=in_specs, out_specs=out_specs, check_vma=False
    )
```

```python
import jax
import jax.numpy as jnp
from jax import lax
from jax.sharding import PartitionSpec as P

CAP = 12288
BLOCK = 768

epsilon = 1e-06
ABSENT = 4.0
OFFSETS = (0, -1, 1, 2)


def shift(x, axis, n, step):
    return lax.ppermute(x, axis, [(i, (i + step) % n) for i in range(n)])


def ring_gather(chunk, axis):
    n = lax.axis_size(axis)
    half = chunk.shape[0] // 2
    from_left = shift(chunk, axis, n, 1)
    from_right = shift(chunk, axis, n, -1)
    far = [shift(from_right[:half], axis, n, -1), shift(from_left[half:], axis, n, 1)]
    return [chunk, from_left, from_right, far]


def block_max(rows, cols, self_block):
    scores = lax.dot_general(
        rows, cols, (((1,), (1,)), ((), ())), preferred_element_type=jnp.float32
    )
    keep = (cols[:, 0].astype(jnp.float32) < 2.0)[None, :]
    if self_block:
        index = jnp.arange(rows.shape[0], dtype=jnp.int32)
        keep = keep & (index[:, None] != index[None, :])
    return jnp.max(jnp.where(keep, scores, -1.0), axis=1)


def on_device(embeddings, target):
    width = embeddings.shape[1]
    clusters_count = lax.axis_size("clus")
    tile_rows = lax.axis_size("trow")
    tile_cols = lax.axis_size("tcol")
    per_cluster = (BLOCK // (clusters_count * tile_rows * tile_cols)) * (CAP // BLOCK)

    values = embeddings.astype(jnp.float32)
    unit_rows = (
        values / jnp.sqrt(jnp.sum(values * values, axis=1, keepdims=True) + epsilon)
    ).astype(jnp.bfloat16)

    cluster = target // CAP
    onehot = (cluster[:, None] == jnp.arange(clusters_count, dtype=jnp.int32)[None, :]).astype(
        jnp.int32
    )
    count = onehot.shape[0]
    earlier = (
        jnp.arange(count, dtype=jnp.int32)[None, :] < jnp.arange(count, dtype=jnp.int32)[:, None]
    ).astype(jnp.bfloat16)
    before = jnp.dot(earlier, onehot.astype(jnp.bfloat16), preferred_element_type=jnp.float32)
    position = jnp.sum(onehot * before.astype(jnp.int32), axis=1)
    slot = cluster * per_cluster + position
    placed = slot[None, :] == jnp.arange(clusters_count * per_cluster, dtype=jnp.int32)[:, None]
    gathered = jnp.dot(
        placed.astype(jnp.bfloat16), unit_rows, preferred_element_type=jnp.float32
    ).astype(jnp.bfloat16)
    outgoing = jnp.where(jnp.any(placed, axis=1)[:, None], gathered, jnp.bfloat16(ABSENT))
    arrived = lax.all_to_all(
        outgoing.reshape(clusters_count, per_cluster, width),
        "clus",
        split_axis=0,
        concat_axis=0,
        tiled=True,
    ).reshape(clusters_count * per_cluster, width)

    row_chunks = ring_gather(arrived, "tcol")
    col_chunks = ring_gather(arrived, "trow")
    col_chunks[-1] = jnp.concatenate(col_chunks[-1], axis=0)
    row_pieces = row_chunks[:-1] + [row_chunks[-1]]

    def row_best(a, rows):
        return jnp.max(
            jnp.stack(
                [block_max(rows, cols, a == 0 and b == 0) for b, cols in enumerate(col_chunks)]
            ),
            axis=0,
        )

    partial = jnp.stack(
        [row_best(a, rows) for a, rows in enumerate(row_chunks[:-1])]
        + [jnp.concatenate([row_best(3, rows) for rows in row_chunks[-1]])]
    )

    own_best = jnp.max(
        jnp.stack(
            [partial[0]]
            + [
                shift(partial[j], "tcol", tile_cols, OFFSETS[j])
                for j in range(1, len(OFFSETS))
            ]
        ),
        axis=0,
    )
    best = lax.all_to_all(
        own_best.reshape(clusters_count, per_cluster),
        "clus",
        split_axis=0,
        concat_axis=0,
        tiled=True,
    )
    owned = (cluster[:, None, None] == jnp.arange(clusters_count)[None, :, None]) & (
        position[:, None, None] == jnp.arange(per_cluster)[None, None, :]
    )
    return jnp.max(jnp.where(owned, best[None], -jnp.inf), axis=(1, 2))


def solution(mesh):
    in_specs = (P(("clus", "trow", "tcol"), None), P(("clus", "trow", "tcol")))
    out_specs = P(("clus", "trow", "tcol"))
    return jax.shard_map(
        on_device, mesh=mesh, in_specs=in_specs, out_specs=out_specs, check_vma=False
    )
```

```python
import jax
import jax.numpy as jnp
from jax import lax
from jax.sharding import PartitionSpec as P

CAP = 12288
BLOCK = 768

epsilon = 1e-06
ABSENT = 4.0
OFFSETS = (0, -1, 1, 2)


def shift(x, axis, n, step):
    return lax.ppermute(x, axis, [(i, (i + step) % n) for i in range(n)])


def ring_gather(chunk, axis):
    n = lax.axis_size(axis)
    half = chunk.shape[0] // 2
    from_left = shift(chunk, axis, n, 1)
    from_right = shift(chunk, axis, n, -1)
    far = [shift(from_right[:half], axis, n, -1), shift(from_left[half:], axis, n, 1)]
    return [chunk, from_left, from_right, far]


def block_max(rows, cols, self_block):
    scores = lax.dot_general(
        rows, cols, (((1,), (1,)), ((), ())), preferred_element_type=jnp.float32
    )
    keep = (cols[:, 0].astype(jnp.float32) < 2.0)[None, :]
    if self_block:
        index = jnp.arange(rows.shape[0], dtype=jnp.int32)
        keep = keep & (index[:, None] != index[None, :])
    return jnp.max(jnp.where(keep, scores, -1.0), axis=1)


def on_device(embeddings, target):
    width = embeddings.shape[1]
    clusters_count = lax.axis_size("clus")
    tile_rows = lax.axis_size("trow")
    tile_cols = lax.axis_size("tcol")
    per_cluster = (BLOCK // (clusters_count * tile_rows * tile_cols)) * (CAP // BLOCK)

    values = embeddings.astype(jnp.float32)
    unit_rows = (
        values / jnp.sqrt(jnp.sum(values * values, axis=1, keepdims=True) + epsilon)
    ).astype(jnp.bfloat16)

    cluster = target // CAP
    onehot = (cluster[:, None] == jnp.arange(clusters_count, dtype=jnp.int32)[None, :]).astype(
        jnp.int32
    )
    count = onehot.shape[0]
    earlier = (
        jnp.arange(count, dtype=jnp.int32)[None, :] < jnp.arange(count, dtype=jnp.int32)[:, None]
    ).astype(jnp.bfloat16)
    before = jnp.dot(earlier, onehot.astype(jnp.bfloat16), preferred_element_type=jnp.float32)
    position = jnp.sum(onehot * before.astype(jnp.int32), axis=1)
    slot = cluster * per_cluster + position
    placed = slot[None, :] == jnp.arange(clusters_count * per_cluster, dtype=jnp.int32)[:, None]
    gathered = jnp.dot(
        placed.astype(jnp.bfloat16), unit_rows, preferred_element_type=jnp.float32
    ).astype(jnp.bfloat16)
    outgoing = jnp.where(jnp.any(placed, axis=1)[:, None], gathered, jnp.bfloat16(ABSENT))
    arrived = lax.all_to_all(
        outgoing.reshape(clusters_count, per_cluster, width),
        "clus",
        split_axis=0,
        concat_axis=0,
        tiled=True,
    ).reshape(clusters_count * per_cluster, width)

    row_chunks = ring_gather(arrived, "tcol")
    col_chunks = ring_gather(arrived, "trow")
    col_chunks = col_chunks[:-1] + list(col_chunks[-1])

    def row_best(a, rows):
        return jnp.max(
            jnp.stack(
                [block_max(rows, cols, a == 0 and b == 0) for b, cols in enumerate(col_chunks)]
            ),
            axis=0,
        )

    partial = jnp.stack(
        [row_best(a, rows) for a, rows in enumerate(row_chunks[:-1])]
        + [jnp.concatenate([row_best(3, rows) for rows in row_chunks[-1]])]
    )

    own_best = jnp.max(
        jnp.stack(
            [partial[0]]
            + [
                shift(partial[j], "tcol", tile_cols, OFFSETS[j])
                for j in range(1, len(OFFSETS))
            ]
        ),
        axis=0,
    )
    best = lax.all_to_all(
        own_best.reshape(clusters_count, per_cluster),
        "clus",
        split_axis=0,
        concat_axis=0,
        tiled=True,
    )
    owned = (cluster[:, None, None] == jnp.arange(clusters_count)[None, :, None]) & (
        position[:, None, None] == jnp.arange(per_cluster)[None, None, :]
    )
    return jnp.max(jnp.where(owned, best[None], -jnp.inf), axis=(1, 2))


def solution(mesh):
    in_specs = (P(("clus", "trow", "tcol"), None), P(("clus", "trow", "tcol")))
    out_specs = P(("clus", "trow", "tcol"))
    return jax.shard_map(
        on_device, mesh=mesh, in_specs=in_specs, out_specs=out_specs, check_vma=False
    )
```
